512 devices in a mesh: wide: 64 (over z, x), narrow: 8 (over y, core).
Axes of the slice: x: 4, y: 4, z: 16, core: 2. Of those that a mesh axis runs over, the one named last changes fastest.
Arguments:
- tokens: bfloat16 [128, 8192], P('wide', 'narrow'), may hold values from -6 to 6
- cotangent: bfloat16 [128, 8192], P('wide', 'narrow'), may hold values from -6 to 6
- gate_tiles: bfloat16 [8, 64, 12, 128, 128], P('narrow', 'wide'), may hold values from -0.109375 to 0.109375
- up_tiles: bfloat16 [8, 64, 12, 128, 128], P('narrow', 'wide'), may hold values from -0.109375 to 0.109375
- down_tiles: bfloat16 [8, 64, 12, 128, 128], P('narrow', 'wide'), may hold values from -0.0625 to 0.0625
- kept_slots: int32 [3, 8, 64, 12], P(None, 'narrow', 'wide'), may hold values from 0 to 23, as said below
- kept_counts: int32 [3, 8, 64], P(None, 'narrow', 'wide'), may hold values from 3 to 12, as said below
Outputs:
- layer_out: bfloat16 [128, 8192], P('wide', 'narrow')
- input_grad: bfloat16 [128, 8192], P('wide', 'narrow')
- gate_grad: bfloat16 [8, 64, 12, 128, 128], P('narrow', 'wide')
- up_grad: bfloat16 [8, 64, 12, 128, 128], P('narrow', 'wide')
- down_grad: bfloat16 [8, 64, 12, 128, 128], P('narrow', 'wide')
The draws below stay inside these ranges and needn't reach their ends.
Inputs may be any that keep to these rules, and one draw needn't show every extreme that they name: `kept_slots`: for each matrix and device the first 12 entries are distinct local tile positions. `kept_counts`: for each matrix some device keeps exactly 12 tiles.
All inputs are finite; a program needn't handle non-finite values.
Results may differ from the reference program's by a relative error of at most 0.005.
Values may be sent and summed in bfloat16 or wider, within the bound.
A program may use at most 64 MiB of HBM per device.

```python
import jax
import jax.numpy as jnp
from jax import lax

D = 8192
TILE = 128
HT_DEV = 3
HIDDEN_SIZE = 24576
TOKENS = 128
DT_DEV = 8
LOC = 24
CAP = 12
N_WIDE = 64
N_NARROW = 8


def shuffle_positions(subkey):
    return jax.random.permutation(subkey, LOC)[:CAP]


def draw_kept_slots(key, part):
    subkeys = jax.random.split(jax.random.fold_in(key, 11), 3 * N_NARROW * N_WIDE)
    lists = jax.vmap(shuffle_positions)(subkeys)
    return lists.reshape(3, N_NARROW, N_WIDE, CAP).astype(jnp.int32)


def draw_kept_counts(key, part):
    lowest = max(LOC // 8, 1)
    spread = CAP - lowest + 1
    first = jax.random.randint(jax.random.fold_in(key, 21), (3, N_NARROW * N_WIDE), 0, spread)
    second = jax.random.randint(jax.random.fold_in(key, 22), (3, N_NARROW * N_WIDE), 0, spread)
    counts = lowest + jnp.minimum(first, second)
    chosen = jax.random.randint(jax.random.fold_in(key, 23), (3,), 0, N_NARROW * N_WIDE)
    counts = counts.at[jnp.arange(3), chosen].set(CAP)
    return counts.reshape(3, N_NARROW, N_WIDE).astype(jnp.int32)


def steps_of(key, extent, pieces, smallest, top_value):
    level, own = 1.0, jax.random.fold_in(key, 6)
    for dim, blocks in pieces:
        heights = jnp.exp(jax.random.uniform(jax.random.fold_in(own, dim), (blocks,), jnp.float32, smallest / len(pieces), top_value / len(pieces)))
        level = level * jnp.repeat(heights, extent[dim] // blocks).reshape([-1 if axis == dim else 1 for axis in range(len(extent))])
    return level


def noise(rng, shape, scale, limit, cuts=(), held_as=jnp.bfloat16):
    level = steps_of(rng, shape, cuts, -0.22, 0.18) if cuts else 1.0
    entries = jax.random.normal(rng, shape, jnp.float32) * scale * level
    return jnp.minimum(jnp.maximum(entries, -limit), limit).astype(held_as)


def setup_inputs(seed: int = 0) -> dict:
    key_of = jax.random.split(jax.random.key(seed), 8)
    tokens = noise(key_of[0], (TOKENS, D), 1.0, 6.0, ((0, 64), (1, 8)))
    cotangent = noise(key_of[1], (TOKENS, D), 1.0, 6.0, ((0, 64), (1, 8)))
    gate_tiles = noise(key_of[2], (N_NARROW, N_WIDE, CAP, TILE, TILE), (D // 3) ** -0.5, 0.109375, ((0, 8), (1, 64)))
    up_tiles = noise(key_of[3], (N_NARROW, N_WIDE, CAP, TILE, TILE), (D // 3) ** -0.5, 0.109375, ((0, 8), (1, 64)))
    down_tiles = noise(key_of[4], (N_NARROW, N_WIDE, CAP, TILE, TILE), (HIDDEN_SIZE // 3) ** -0.5, 0.0625, ((0, 8), (1, 64)))
    kept_slots = draw_kept_slots(jax.random.fold_in(key_of[7], 71), 0)
    kept_counts = draw_kept_counts(jax.random.fold_in(key_of[7], 71), 0)
    return {"tokens": tokens, "cotangent": cotangent, "gate_tiles": gate_tiles, "up_tiles": up_tiles, "down_tiles": down_tiles, "kept_slots": kept_slots, "kept_counts": kept_counts}


highest = lax.Precision.HIGHEST

def onehots(slot_list, kept_count, row_tiles, col_tiles):
    row_onehot = (slot_list[:, None] // col_tiles == jnp.arange(row_tiles, dtype=jnp.int32)[None, :]).astype(jnp.float32)
    col_onehot = (slot_list[:, None] % col_tiles == jnp.arange(col_tiles, dtype=jnp.int32)[None, :]).astype(jnp.float32)
    live_mask = (jnp.arange(slot_list.shape[0], dtype=jnp.int32) < kept_count).astype(jnp.float32)
    return (row_onehot, col_onehot, live_mask)

def tile_product(panel_in, tiles, slot_list, kept_count, col_tiles):
    row_onehot, col_onehot, live_mask = onehots(slot_list, kept_count, panel_in.shape[1], col_tiles)
    picked = jnp.einsum('tra,kr->kta', panel_in.astype(jnp.float32), row_onehot, precision=highest)
    product = jnp.einsum('kta,kab->ktb', picked, tiles.astype(jnp.float32), precision=highest)
    return jnp.einsum('ktb,kc->tcb', product, col_onehot * live_mask[:, None], precision=highest)

def tile_transposed(panel_out, tiles, slot_list, kept_count, row_tiles):
    row_onehot, col_onehot, live_mask = onehots(slot_list, kept_count, row_tiles, panel_out.shape[1])
    picked = jnp.einsum('tcb,kc->ktb', panel_out.astype(jnp.float32), col_onehot, precision=highest)
    product = jnp.einsum('ktb,kab->kta', picked, tiles.astype(jnp.float32), precision=highest)
    return jnp.einsum('kta,kr->tra', product, row_onehot * live_mask[:, None], precision=highest)

def tile_grad(panel_in, panel_out, slot_list, kept_count):
    row_onehot, col_onehot, live_mask = onehots(slot_list, kept_count, panel_in.shape[1], panel_out.shape[1])
    picked_in = jnp.einsum('tra,kr->kta', panel_in.astype(jnp.float32), row_onehot, precision=highest)
    picked_out = jnp.einsum('tcb,kc->ktb', panel_out.astype(jnp.float32), col_onehot, precision=highest)
    grads = jnp.einsum('kta,ktb->kab', picked_in, picked_out, precision=highest)
    return (grads * live_mask[:, None, None]).astype(jnp.bfloat16)

def reference(tokens, cotangent, gate_tiles, up_tiles, down_tiles, kept_slots, kept_counts):
    token_blocks = tokens.reshape(TOKENS, N_NARROW, DT_DEV, TILE).transpose(1, 0, 2, 3)
    grad_blocks = cotangent.reshape(TOKENS, N_NARROW, DT_DEV, TILE).transpose(1, 0, 2, 3)

    def gate_column(wide_index):

        def single(narrow_index):
            first = tile_product(token_blocks[narrow_index], gate_tiles[narrow_index, wide_index], kept_slots[0, narrow_index, wide_index], kept_counts[0, narrow_index, wide_index], HT_DEV)
            second = tile_product(token_blocks[narrow_index], up_tiles[narrow_index, wide_index], kept_slots[1, narrow_index, wide_index], kept_counts[1, narrow_index, wide_index], HT_DEV)
            return (first, second)
        firsts, seconds = jax.vmap(single)(jnp.arange(N_NARROW))
        return (lax.optimization_barrier(jnp.sum(firsts, 0)), lax.optimization_barrier(jnp.sum(seconds, 0)))
    gate_sum, up_sum = lax.map(gate_column, jnp.arange(N_WIDE))
    hidden = (jax.nn.silu(gate_sum) * up_sum).astype(jnp.bfloat16)

    def out_block(narrow_index):

        def accumulate(wide_index, carry):
            return carry + tile_product(hidden[wide_index], down_tiles[narrow_index, wide_index], kept_slots[2, narrow_index, wide_index], kept_counts[2, narrow_index, wide_index], DT_DEV)
        return lax.fori_loop(0, N_WIDE, accumulate, jnp.zeros((TOKENS, DT_DEV, TILE), jnp.float32))
    out_sum = lax.map(out_block, jnp.arange(N_NARROW))
    layer_out = out_sum.transpose(1, 0, 2, 3).reshape(TOKENS, D).astype(jnp.bfloat16)

    def hidden_column(wide_index):

        def single(narrow_index):
            return tile_transposed(grad_blocks[narrow_index], down_tiles[narrow_index, wide_index], kept_slots[2, narrow_index, wide_index], kept_counts[2, narrow_index, wide_index], HT_DEV)
        return lax.optimization_barrier(jnp.sum(jax.vmap(single)(jnp.arange(N_NARROW)), 0))
    hidden_grad = lax.map(hidden_column, jnp.arange(N_WIDE))
    sigmoid_gate = jax.nn.sigmoid(gate_sum)
    gate_act = (hidden_grad * up_sum * sigmoid_gate * (1.0 + gate_sum * (1.0 - sigmoid_gate))).astype(jnp.bfloat16)
    up_act = (hidden_grad * gate_sum * sigmoid_gate).astype(jnp.bfloat16)

    def input_block(narrow_index):

        def accumulate(wide_index, carry):
            first = tile_transposed(gate_act[wide_index], gate_tiles[narrow_index, wide_index], kept_slots[0, narrow_index, wide_index], kept_counts[0, narrow_index, wide_index], DT_DEV)
            second = tile_transposed(up_act[wide_index], up_tiles[narrow_index, wide_index], kept_slots[1, narrow_index, wide_index], kept_counts[1, narrow_index, wide_index], DT_DEV)
            return carry + first + second
        return lax.fori_loop(0, N_WIDE, accumulate, jnp.zeros((TOKENS, DT_DEV, TILE), jnp.float32))
    input_sum = lax.map(input_block, jnp.arange(N_NARROW))
    input_grad = input_sum.transpose(1, 0, 2, 3).reshape(TOKENS, D).astype(jnp.bfloat16)

    def grad_row(narrow_index):

        def grad_cell(wide_index):
            first = tile_grad(token_blocks[narrow_index], gate_act[wide_index], kept_slots[0, narrow_index, wide_index], kept_counts[0, narrow_index, wide_index])
            second = tile_grad(token_blocks[narrow_index], up_act[wide_index], kept_slots[1, narrow_index, wide_index], kept_counts[1, narrow_index, wide_index])
            third = tile_grad(hidden[wide_index], grad_blocks[narrow_index], kept_slots[2, narrow_index, wide_index], kept_counts[2, narrow_index, wide_index])
            return (first, second, third)
        return lax.map(grad_cell, jnp.arange(N_WIDE))
    gate_grad, up_grad, down_grad = lax.map(grad_row, jnp.arange(N_NARROW))
    return (layer_out, input_grad, gate_grad, up_grad, down_grad)
```

```python
import functools

import jax
import jax.numpy as jnp
from jax import lax
from jax.experimental import pallas as pl
from jax.experimental.pallas import tpu as pltpu
from jax.sharding import PartitionSpec as P

TILE = 128
HT = 3
DT = 8
LOC = HT * DT
X_SIZE = 4
REACH = 2
F32, BF16 = jnp.float32, jnp.bfloat16
MESH = pl.DeviceIdType.MESH


def layer_kernel(
    nz, nx, nn, cap,
    slots, counts, tok_hbm, cot_hbm, gate_hbm, up_hbm, down_hbm,
    layer_out, input_grad, gate_grad, up_grad, down_grad,
    own_in, pair, gathered, tiles, w_in, w_down, rows, tok, cot, tok_t, hid_t, act,
    part, part_in, acts, back, back_in, back_sum, last_in, grads,
    sem_in, sem_out, zs, zr, xs, xr, ps, pr, as_, ar, bs, br, ls, lr,
):
    wide, me = lax.axis_index("wide"), lax.axis_index("narrow")
    z, x = wide // nx, wide % nx
    half = nz // 2
    width = HT * TILE
    tokens = 2 * nz * nx
    own_rows = tokens // nn
    per_z = 2 * nx

    def at_z(step):
        return ((z + step + nz) % nz * nx + x, me)

    def at_x(step):
        return (z * nx + (x + step) % nx, me)

    def at_n(step):
        return (wide, (me + step) % nn)

    def remote(src, dst, send, recv, target):
        return pltpu.make_async_remote_copy(
            src_ref=src, dst_ref=dst, send_sem=send, recv_sem=recv,
            device_id=target, device_id_type=MESH,
        )

    loads = [
        pltpu.make_async_copy(tok_hbm, own_in.at[0], sem_in.at[0]),
        pltpu.make_async_copy(cot_hbm, own_in.at[1], sem_in.at[1]),
        pltpu.make_async_copy(gate_hbm, tiles.at[0], sem_in.at[2]),
        pltpu.make_async_copy(up_hbm, tiles.at[1], sem_in.at[3]),
        pltpu.make_async_copy(down_hbm, tiles.at[2], sem_in.at[4]),
    ]
    for load in loads:
        load.start()

    barrier = pltpu.get_barrier_semaphore()
    z_near = sorted({s % nz for d in range(1, REACH + 1) for s in (d, -d)})
    for step in z_near:
        pl.semaphore_signal(barrier, inc=1, device_id=at_z(step), device_id_type=MESH)
    for step in range(1, nx):
        pl.semaphore_signal(barrier, inc=1, device_id=at_x(step), device_id_type=MESH)
    for step in range(1, nn):
        pl.semaphore_signal(barrier, inc=1, device_id=at_n(step), device_id_type=MESH)

    loads[0].wait()
    loads[1].wait()
    for o in range(2):
        both = own_in[o].astype(F32)
        for k in range(DT):
            for i in range(2):
                pair[o, pl.ds(8 * i + k, 1), :] = both[i : i + 1, k * TILE : (k + 1) * TILE]
        gathered[x, 0, o] = pair[o].astype(BF16)

    pl.semaphore_wait(barrier, len(z_near) + nx - 1 + nn - 1)

    def z_copy(slot, to_slot, step):
        return remote(
            gathered.at[x, slot], gathered.at[x, to_slot],
            zs.at[to_slot], zr.at[to_slot], at_z(step),
        )

    def x_copy(slot, step):
        return remote(
            gathered.at[x, slot], gathered.at[x, slot],
            xs.at[step - 1, slot], xr.at[step - 1, slot], at_x(step),
        )

    for d in range(1, REACH + 1):
        z_copy(0, nz - d, d).start()
        if d < half:
            z_copy(0, d, -d).start()
    for step in range(1, nx):
        x_copy(0, step).start()

    def relay(d, carry):
        up = nz - d
        z_copy(up, up, 0).wait_recv()

        @pl.when(d + REACH <= half)
        def _():
            z_copy(up, up - REACH, REACH).start()

        for step in range(1, nx):
            x_copy(up, step).start()

        @pl.when(d < half)
        def _():
            z_copy(d, d, 0).wait_recv()

            @pl.when(d + REACH < half)
            def _():
                z_copy(d, d + REACH, -REACH).start()

            for step in range(1, nx):
                x_copy(d, step).start()

        return carry

    for load in loads[2:]:
        load.wait()

    def place(p, carry):
        for m in range(3):
            found, live = jnp.int32(0), jnp.int32(0)
            for s in range(cap):
                hit = jnp.logical_and(slots[m, 0, 0, s] == p, s < counts[m, 0, 0])
                found = jnp.where(hit, s, found)
                live = jnp.where(hit, 1, live)
            tile = (tiles[m, found].astype(F32) * live.astype(F32)).astype(BF16)
            if m < 2:
                w_in[
                    pl.ds(pl.multiple_of(p // HT * TILE, TILE), TILE),
                    pl.ds(pl.multiple_of(p % HT * TILE + m * width, TILE), TILE),
                ] = tile
            else:
                w_down[
                    pl.ds(pl.multiple_of(p // DT * TILE, TILE), TILE),
                    pl.ds(pl.multiple_of(p % DT * TILE, TILE), TILE),
                ] = tile
        return carry

    lax.fori_loop(1, half // 2 + 1, relay, 0)
    lax.fori_loop(0, LOC, place, 0)
    lax.fori_loop(half // 2 + 1, half + 1, relay, 0)

    def x_arrival(slot, carry):
        for step in range(1, nx):
            x_copy(slot, step).wait_recv()
        return carry

    lax.fori_loop(0, nz, x_arrival, 0)

    def unpack(slot, carry):
        for o in range(2):
            for xx in range(nx):
                at = pl.multiple_of(slot * 8 * per_z + xx * 16, 16)
                rows[o, pl.ds(at, 16), :] = gathered[xx, slot, o].astype(F32)
        return carry

    lax.fori_loop(0, nz, unpack, 0)
    for k in range(DT):
        tok[:, k * TILE : (k + 1) * TILE] = rows[0, pl.ds(k, tokens, stride=8), :].astype(BF16)
        cot[k] = rows[1, pl.ds(k, tokens, stride=8), :].astype(BF16)

    gate_up = jnp.dot(tok[...], w_in[...], preferred_element_type=F32)
    part[:, :, : 2 * width] = gate_up.astype(BF16).reshape(nn, own_rows, 2 * width)
    hid = jnp.zeros((tokens, width), F32)
    for k in range(DT):
        hid = hid + lax.dot_general(
            cot[k], w_down[:, k * TILE : (k + 1) * TILE],
            (((1,), (1,)), ((), ())), preferred_element_type=F32,
        )
    part[:, :, 2 * width :] = hid.astype(BF16).reshape(nn, own_rows, width)

    def p_copy(step):
        return remote(
            part.at[(me + step) % nn], part_in.at[step],
            ps.at[step], pr.at[step], at_n(step),
        )

    for step in range(1, nn):
        p_copy(step).start()

    for k in range(DT):
        tok_t[k] = rows[0, pl.ds(k, tokens, stride=8), :].T.astype(BF16)

    total = part[me].astype(F32)
    for step in range(1, nn):
        p_copy(step).wait_recv()
        total = total + part_in[step].astype(F32)
    gate_sum, up_sum = total[:, :width], total[:, width : 2 * width]
    hidden_grad = total[:, 2 * width :]
    sig = jax.nn.sigmoid(gate_sum)
    acts[me, :, :width] = (gate_sum * sig * up_sum).astype(BF16)
    acts[me, :, width : 2 * width] = (
        hidden_grad * up_sum * sig * (1.0 + gate_sum * (1.0 - sig))
    ).astype(BF16)
    acts[me, :, 2 * width :] = (hidden_grad * gate_sum * sig).astype(BF16)

    def a_copy(step):
        return remote(
            acts.at[me], acts.at[me], as_.at[step], ar.at[step], at_n(step),
        )

    for step in range(1, nn):
        a_copy(step).start()
    for step in range(1, nn):
        a_copy(step).wait_recv()

    everything = acts[...].reshape(tokens, 3 * width)
    out = jnp.dot(everything[:, :width], w_down[...], preferred_element_type=F32)
    for k in range(DT):
        rows[0, pl.ds(k, tokens, stride=8), :] = out[:, k * TILE : (k + 1) * TILE]
    both_act = everything[:, width:]
    for k in range(DT):
        rows[1, pl.ds(k, tokens, stride=8), :] = lax.dot_general(
            both_act, w_in[k * TILE : (k + 1) * TILE, :],
            (((1,), (1,)), ((), ())), preferred_element_type=F32,
        )

    def b_copy(slot, step):
        return remote(
            back.at[(x + step) % nx, slot], back_in.at[step - 1, slot],
            bs.at[step - 1, slot], br.at[step - 1, slot], at_x(step),
        )

    def far_first(q):
        d = half - (q + 1) // 2
        return jnp.where(q % 2 == 1, d, (nz - d) % nz)

    def to_x(q, carry):
        slot = far_first(q)
        for o in range(2):
            for xx in range(nx):
                at = pl.multiple_of(slot * 8 * per_z + xx * 16, 16)
                back[xx, slot, o] = rows[o, pl.ds(at, 16), :].astype(BF16)
        for step in range(1, nx):
            b_copy(slot, step).start()
        return carry

    lax.fori_loop(0, nz, to_x, 0)

    def l_copy(slot, step):
        return remote(
            back_sum.at[slot], last_in.at[(nz - slot) % nz],
            ls.at[slot], lr.at[(nz - slot) % nz], at_z(step),
        )

    def to_z(q, carry):
        slot = far_first(q)
        for step in range(1, nx):
            b_copy(slot, step).wait_recv()
        summed = back[x, slot].astype(F32)
        for step in range(1, nx):
            summed = summed + back_in[step - 1, slot].astype(F32)
        back_sum[slot] = summed.astype(BF16)

        @pl.when(q < nz - 1)
        def _():
            l_copy(slot, slot).start()

        return carry

    lax.fori_loop(0, nz, to_z, 0)

    for j in range(3 * HT):
        act[j] = everything[:, j * TILE : (j + 1) * TILE]
    for j in range(HT):
        hid_t[j] = act[j].astype(F32).T.astype(BF16)
    stores = []
    for m, to in ((0, gate_grad), (1, up_grad), (2, down_grad)):

        def tile_grad(s, carry):
            p = slots[m, 0, 0, s]
            if m < 2:
                left, right = tok_t[p // HT], act[HT * (m + 1) + p % HT]
            else:
                left, right = hid_t[p // DT], cot[p % DT]
            grad = jnp.dot(left, right, preferred_element_type=F32)
            live = (s < counts[m, 0, 0]).astype(F32)
            grads[m, s] = (grad * live).astype(BF16)
            return carry

        lax.fori_loop(0, cap, tile_grad, 0)
        store = pltpu.make_async_copy(grads.at[m], to, sem_out.at[m])
        store.start()
        stores.append(store)

    def last(slot, carry):
        l_copy((nz - slot) % nz, 0).wait_recv()
        return carry + last_in[slot].astype(F32)

    final = lax.fori_loop(1, nz, last, back_sum[0].astype(F32))
    for o, to in ((0, layer_out), (1, input_grad)):
        pair[o] = final[o]
        for k in range(DT):
            for i in range(2):
                to[i : i + 1, k * TILE : (k + 1) * TILE] = pair[
                    o, pl.ds(8 * i + k, 1), :
                ].astype(BF16)

    def sent_x(slot, carry):
        for step in range(1, nx):
            x_copy(slot, step).wait_send()
            b_copy(slot, step).wait_send()
        return carry

    lax.fori_loop(0, nz, sent_x, 0)

    def sent_z(slot, carry):
        z_copy(slot, slot, 0).wait_send()
        l_copy(slot, 0).wait_send()
        return carry

    lax.fori_loop(1, nz, sent_z, 0)
    for step in range(1, nn):
        p_copy(step).wait_send()
        a_copy(step).wait_send()
    for store in stores:
        store.wait()


def per_device(nz, nx, nn, tokens, cotangent, gate_tiles, up_tiles, down_tiles, slots, counts):
    cap = gate_tiles.shape[2]
    count = 2 * nz * nx
    own = count // nn
    block = (cap, TILE, TILE)
    width = HT * TILE
    features = DT * TILE
    dma = pltpu.SemaphoreType.DMA
    vmem = pltpu.VMEM
    anywhere = pl.BlockSpec(memory_space=pl.ANY)
    smem = pl.BlockSpec(memory_space=pltpu.SMEM)
    in_vmem = pl.BlockSpec(memory_space=pltpu.VMEM)
    results = pl.pallas_call(
        functools.partial(layer_kernel, nz, nx, nn, cap),
        out_shape=(
            jax.ShapeDtypeStruct(tokens.shape, BF16),
            jax.ShapeDtypeStruct(tokens.shape, BF16),
            jax.ShapeDtypeStruct(block, BF16),
            jax.ShapeDtypeStruct(block, BF16),
            jax.ShapeDtypeStruct(block, BF16),
        ),
        in_specs=[smem, smem] + [anywhere] * 5,
        out_specs=(in_vmem, in_vmem, anywhere, anywhere, anywhere),
        scratch_shapes=[
            vmem((2, 2, features), BF16),
            vmem((2, 16, TILE), F32),
            vmem((nx, nz, 2, 16, TILE), BF16),
            vmem((3, *block), BF16),
            vmem((features, 2 * width), BF16),
            vmem((width, features), BF16),
            vmem((2, count * 8, TILE), F32),
            vmem((count, features), BF16),
            vmem((DT, count, TILE), BF16),
            vmem((DT, TILE, count), BF16),
            vmem((HT, TILE, count), BF16),
            vmem((3 * HT, count, TILE), BF16),
            vmem((nn, own, 3 * width), BF16),
            vmem((nn, own, 3 * width), BF16),
            vmem((nn, own, 3 * width), BF16),
            vmem((nx, nz, 2, 16, TILE), BF16),
            vmem((nx - 1, nz, 2, 16, TILE), BF16),
            vmem((nz, 2, 16, TILE), BF16),
            vmem((nz, 2, 16, TILE), BF16),
            vmem((3, *block), BF16),
            dma((5,)),
            dma((3,)),
            dma((nz,)),
            dma((nz,)),
            dma((nx - 1, nz)),
            dma((nx - 1, nz)),
            dma((nn,)),
            dma((nn,)),
            dma((nn,)),
            dma((nn,)),
            dma((nx - 1, nz)),
            dma((nx - 1, nz)),
            dma((nz,)),
            dma((nz,)),
        ],
        compiler_params=pltpu.CompilerParams(collective_id=0, has_side_effects=True),
        name="pruned_layer",
    )(
        slots, counts, tokens, cotangent,
        gate_tiles.reshape(block), up_tiles.reshape(block), down_tiles.reshape(block),
    )
    layer_out, input_grad, *tile_grads = results
    return (layer_out, input_grad, *(g[None, None] for g in tile_grads))


def solution(mesh, x_size=X_SIZE):
    tiles = P("narrow", "wide", None, None, None)
    panel = P("wide", "narrow")
    wide, narrow = mesh.shape["wide"], mesh.shape["narrow"]
    return jax.shard_map(
        functools.partial(per_device, wide // x_size, x_size, narrow),
        mesh=mesh,
        in_specs=(
            panel, panel, tiles, tiles, tiles,
            P(None, "narrow", "wide", None), P(None, "narrow", "wide"),
        ),
        out_specs=(panel, panel, tiles, tiles, tiles),
        check_vma=False,
    )
```

```python
import functools

import jax
import jax.numpy as jnp
from jax import lax
from jax.experimental import pallas as pl
from jax.experimental.pallas import tpu as pltpu
from jax.sharding import PartitionSpec as P

TILE = 128
HT = 3
DT = 8
LOC = HT * DT
X_SIZE = 4
VMEM_LIMIT = 24 * 1024 * 1024
F32, BF16 = jnp.float32, jnp.bfloat16
MESH = pl.DeviceIdType.MESH


def layer_kernel(
    nz, nx, nn, cap,
    slots_hbm, counts_hbm, tok_hbm, cot_hbm, gate_hbm, up_hbm, down_hbm,
    layer_out, input_grad, grads,
    slots, counts, own_in, pair, gathered, tiles, keys, w_in, w_down, rows, rows_out,
    tok, cot, tok_t, hid_t, act,
    part_own, part, part_in, acts, back, back_in, back_sum, last_in,
    sem_in, zs, zr, xs, xr, ps, pr, as_, ar, bs, br, ls, lr,
):
    wide, me = lax.axis_index("wide"), lax.axis_index("narrow")
    z, x = wide // nx, wide % nx
    half, reach = nz // 2, nz // 4
    width = HT * TILE
    features = DT * TILE
    tokens = 2 * nz * nx
    per_z = 2 * nx
    in_chunk = tokens // 2
    own_rows = in_chunk // nn
    home = reach - 1

    def at_z(step):
        return ((z + step + nz) % nz * nx + x, me)

    def at_x(step):
        return (z * nx + (x + step) % nx, me)

    def at_n(step):
        return (wide, (me + step) % nn)

    def slot_of(step):
        return (home + step + nz) % nz

    def remote(src, dst, send, recv, target):
        return pltpu.make_async_remote_copy(
            src_ref=src, dst_ref=dst, send_sem=send, recv_sem=recv,
            device_id=target, device_id_type=MESH,
        )

    barrier = pltpu.get_barrier_semaphore()
    z_near = sorted({s % nz for d in range(1, reach + 1) for s in (d, -d)})
    for step in z_near:
        pl.semaphore_signal(barrier, inc=1, device_id=at_z(step), device_id_type=MESH)
    for step in range(1, nx):
        pl.semaphore_signal(barrier, inc=1, device_id=at_x(step), device_id_type=MESH)
    for step in range(1, nn):
        pl.semaphore_signal(barrier, inc=1, device_id=at_n(step), device_id_type=MESH)

    loads = [
        pltpu.make_async_copy(tok_hbm, own_in.at[0], sem_in.at[0]),
        pltpu.make_async_copy(cot_hbm, own_in.at[1], sem_in.at[1]),
        pltpu.make_async_copy(gate_hbm, tiles.at[0], sem_in.at[2]),
        pltpu.make_async_copy(up_hbm, tiles.at[1], sem_in.at[3]),
        pltpu.make_async_copy(down_hbm, tiles.at[2], sem_in.at[4]),
        pltpu.make_async_copy(slots_hbm, slots, sem_in.at[5]),
        pltpu.make_async_copy(counts_hbm, counts, sem_in.at[6]),
    ]
    for load in loads:
        load.start()

    loads[0].wait()
    loads[1].wait()
    for o in range(2):
        both = own_in[o].astype(F32)
        for k in range(DT):
            for i in range(2):
                pair[o, pl.ds(8 * i + k, 1), :] = both[i : i + 1, k * TILE : (k + 1) * TILE]
        gathered[x, home, o] = pair[o].astype(BF16)

    pl.semaphore_wait(barrier, len(z_near) + nx - 1 + nn - 1)

    def z_copy(slot, step):
        to_slot = (slot - step + nz) % nz
        return remote(
            gathered.at[x, slot], gathered.at[x, to_slot],
            zs.at[to_slot], zr.at[to_slot], at_z(step),
        )

    def z_arrival(slot):
        return remote(
            gathered.at[x, slot], gathered.at[x, slot], zs.at[slot], zr.at[slot], at_z(1),
        )

    def x_copy(slot, step):
        return remote(
            gathered.at[x, slot], gathered.at[x, slot],
            xs.at[step - 1, slot], xr.at[step - 1, slot], at_x(step),
        )

    for d in range(1, reach + 1):
        z_copy(home, d).start()
        z_copy(home, -d).start()
    for step in range(1, nx):
        x_copy(home, step).start()

    def relay(d, carry):
        behind = slot_of(-d)
        z_arrival(behind).wait_recv()

        @pl.when(d + reach <= half)
        def _():
            z_copy(behind, reach).start()

        @pl.when(d < half)
        def _():
            ahead = slot_of(d)
            z_arrival(ahead).wait_recv()

            @pl.when(d + reach < half)
            def _():
                z_copy(ahead, -reach).start()

            for step in range(1, nx):
                x_copy(ahead, step).start()

        for step in range(1, nx):
            x_copy(behind, step).start()
        return carry

    for load in loads[2:]:
        load.wait()
    for m in range(3):
        for s in range(cap):
            keys[m, s] = jnp.where(s < counts[0, 0, m], slots[m, 0, 0, s], -1)

    def place(m, p, carry):
        found = jnp.int32(-1)
        for s in range(cap):
            found = jnp.where(keys[m, s] == p, s, found)
        live = found >= 0
        tile = tiles[m, jnp.where(live, found, 0)]
        tile = jnp.where(live, tile, jnp.zeros_like(tile))
        if m < 2:
            w_in[
                pl.ds(pl.multiple_of(p // HT * TILE, TILE), TILE),
                pl.ds(pl.multiple_of(p % HT * TILE + m * width, TILE), TILE),
            ] = tile
        else:
            w_down[
                pl.ds(pl.multiple_of(p // DT * TILE, TILE), TILE),
                pl.ds(pl.multiple_of(p % DT * TILE, TILE), TILE),
            ] = tile
        return carry

    def unpack(c):
        def one(slot, carry):
            for step in range(1, nx):
                x_copy(slot, step).wait_recv()
            for o in range(2):
                for xx in range(nx):
                    at = pl.multiple_of(slot * 8 * per_z + xx * 16, 16)
                    rows[o, pl.ds(at, 16), :] = gathered[xx, slot, o].astype(F32)
            return carry

        lax.fori_loop(c * half, (c + 1) * half, one, 0)
        here = pl.ds(c * in_chunk, in_chunk)
        for k in range(DT):
            picked = pl.ds(c * in_chunk * 8 + k, in_chunk, stride=8)
            tok[here, k * TILE : (k + 1) * TILE] = rows[0, picked, :].astype(BF16)
            cot[k, here, :] = rows[1, picked, :].astype(BF16)

    def p_copy(c, step):
        return remote(
            part.at[c, (me + step) % nn], part_in.at[c, step],
            ps.at[c, step], pr.at[c, step], at_n(step),
        )

    def front(c):
        here = pl.ds(c * in_chunk, in_chunk)
        gate_up = jnp.dot(tok[here, :], w_in[...], preferred_element_type=F32)
        hid = jnp.zeros((in_chunk, width), F32)
        for k in range(DT):
            hid = hid + lax.dot_general(
                cot[k, here, :], w_down[:, k * TILE : (k + 1) * TILE],
                (((1,), (1,)), ((), ())), preferred_element_type=F32,
            )
        for value, at in ((gate_up, 0), (hid, 2 * width)):
            value = value.reshape(nn, own_rows, value.shape[1])
            part_own[c, :, :, at : at + value.shape[2]] = value
            part[c, :, :, at : at + value.shape[2]] = value.astype(BF16)
        for step in range(1, nn):
            p_copy(c, step).start()

    def a_copy(c, step):
        return remote(
            acts.at[c, me], acts.at[c, me], as_.at[c, step], ar.at[c, step], at_n(step),
        )

    def middle(c):
        total = part_own[c, me]
        for step in range(1, nn):
            p_copy(c, step).wait_recv()
            total = total + part_in[c, step].astype(F32)
        gate_sum, up_sum = total[:, :width], total[:, width : 2 * width]
        hidden_grad = total[:, 2 * width :]
        sig = jax.nn.sigmoid(gate_sum)
        acts[c, me, :, :width] = (gate_sum * sig * up_sum).astype(BF16)
        acts[c, me, :, width : 2 * width] = (
            hidden_grad * up_sum * sig * (1.0 + gate_sum * (1.0 - sig))
        ).astype(BF16)
        acts[c, me, :, 2 * width :] = (hidden_grad * gate_sum * sig).astype(BF16)
        for step in range(1, nn):
            a_copy(c, step).start()

    def b_copy(slot, step):
        return remote(
            back.at[(x + step) % nx, slot], back_in.at[step - 1, slot],
            bs.at[step - 1, slot], br.at[step - 1, slot], at_x(step),
        )

    def far_first(c, q):
        d = half - c_start(c) - (q + 1) // 2
        return slot_of(jnp.where(q % 2 == 0, d, nz - d))

    def c_start(c):
        return 0 if c else reach

    def finish(c):
        here = pl.ds(c * in_chunk, in_chunk)
        for step in range(1, nn):
            a_copy(c, step).wait_recv()
        everything = acts[c].astype(F32).reshape(in_chunk, 3 * width).astype(BF16)
        for j in range(3 * HT):
            act[j, here, :] = everything[:, j * TILE : (j + 1) * TILE]
        out = jnp.dot(everything[:, :width], w_down[...], preferred_element_type=F32)
        both_act = everything[:, width:]
        for k in range(DT):
            picked = pl.ds(c * in_chunk * 8 + k, in_chunk, stride=8)
            rows_out[0, picked, :] = out[:, k * TILE : (k + 1) * TILE]
            rows_out[1, picked, :] = lax.dot_general(
                both_act, w_in[k * TILE : (k + 1) * TILE, :],
                (((1,), (1,)), ((), ())), preferred_element_type=F32,
            )

        def to_x(q, carry):
            slot = far_first(c, q)
            for o in range(2):
                for xx in range(nx):
                    at = pl.multiple_of(slot * 8 * per_z + xx * 16, 16)
                    back[xx, slot, o] = rows_out[o, pl.ds(at, 16), :].astype(BF16)
            for step in range(1, nx):
                b_copy(slot, step).start()
            return carry

        lax.fori_loop(0, half, to_x, 0)

    def l_copy(slot):
        step = slot - home
        to_slot = slot_of(-step)
        return remote(
            back_sum.at[slot], last_in.at[to_slot], ls.at[slot], lr.at[to_slot], at_z(step),
        )

    def l_arrival(slot):
        return remote(
            back_sum.at[slot], last_in.at[slot], ls.at[slot], lr.at[slot], at_z(1),
        )

    def summed_over_x(slot):
        for step in range(1, nx):
            b_copy(slot, step).wait_recv()
        at = pl.multiple_of(slot * 8 * per_z + x * 16, 16)
        total = rows_out[:, pl.ds(at, 16), :]
        for step in range(1, nx):
            total = total + back_in[step - 1, slot].astype(F32)
        return total

    def to_z(c):
        def one(q, carry):
            slot = far_first(c, q)
            back_sum[slot] = summed_over_x(slot).astype(BF16)
            l_copy(slot).start()
            return carry

        lax.fori_loop(0, half if c else half - 1, one, 0)

    split = reach + (half - reach) // 2
    lax.fori_loop(0, LOC // 2, functools.partial(place, 0), 0)
    lax.fori_loop(1, reach + 1, relay, 0)
    lax.fori_loop(LOC // 2, LOC, functools.partial(place, 0), 0)
    lax.fori_loop(0, LOC, functools.partial(place, 1), 0)
    lax.fori_loop(0, LOC, functools.partial(place, 2), 0)
    lax.fori_loop(reach + 1, split + 1, relay, 0)
    unpack(0)
    front(0)
    lax.fori_loop(split + 1, half + 1, relay, 0)
    middle(0)
    unpack(1)
    front(1)
    finish(0)
    middle(1)
    to_z(0)
    for k in range(DT):
        tok_t[k] = rows[0, pl.ds(k, tokens, stride=8), :].T.astype(BF16)
    finish(1)
    to_z(1)

    for j in range(HT):
        hid_t[j] = act[j].astype(F32).T.astype(BF16)
    for m in range(3):

        def tile_grad(s, carry):
            p = slots[m, 0, 0, s]
            if m < 2:
                left, right = tok_t[p // HT], act[HT * (m + 1) + p % HT]
            else:
                left, right = hid_t[p // DT], cot[p % DT]
            grad = jnp.dot(left, right, preferred_element_type=F32)
            live = (s < counts[0, 0, m]).astype(F32)
            grads[m, s] = (grad * live).astype(BF16)
            return carry

        lax.fori_loop(0, cap, tile_grad, 0, unroll=4)

    def last(slot, carry):
        l_arrival(slot).wait_recv()
        return carry + last_in[slot].astype(F32)

    final = lax.fori_loop(0, home, last, summed_over_x(home))
    final = lax.fori_loop(home + 1, nz, last, final)
    for o, to in ((0, layer_out), (1, input_grad)):
        pair[o] = final[o]
        for k in range(DT):
            for i in range(2):
                to[i : i + 1, k * TILE : (k + 1) * TILE] = pair[
                    o, pl.ds(8 * i + k, 1), :
                ].astype(BF16)

    def sent(slot, carry):
        for step in range(1, nx):
            x_copy(slot, step).wait_send()
            b_copy(slot, step).wait_send()

        @pl.when(slot != home)
        def _():
            z_arrival(slot).wait_send()
            l_copy(slot).wait_send()

        return carry

    lax.fori_loop(0, nz, sent, 0)
    for c in range(2):
        for step in range(1, nn):
            p_copy(c, step).wait_send()
            a_copy(c, step).wait_send()


def write_kernel(*refs):
    sems = refs[-1]
    layer_out, input_grad, grads, *outs = refs[:-1]
    sources = (layer_out, input_grad, grads.at[0], grads.at[1], grads.at[2])
    stores = [
        pltpu.make_async_copy(source, to, sems.at[i])
        for i, (source, to) in enumerate(zip(sources, outs))
    ]
    for store in stores:
        store.start()
    for store in stores:
        store.wait()


def per_device(nz, nx, nn, tokens, cotangent, gate_tiles, up_tiles, down_tiles, slots, counts):
    cap = gate_tiles.shape[2]
    count = 2 * nz * nx
    own = count // 2 // nn
    block = (cap, TILE, TILE)
    width = HT * TILE
    features = DT * TILE
    dma = pltpu.SemaphoreType.DMA
    vmem = pltpu.VMEM
    anywhere = pl.BlockSpec(memory_space=pl.ANY)
    in_hbm = pl.BlockSpec(memory_space=pltpu.HBM)
    in_vmem = pl.BlockSpec(memory_space=pltpu.VMEM)
    results = pl.pallas_call(
        functools.partial(layer_kernel, nz, nx, nn, cap),
        out_shape=(
            vmem(tokens.shape, BF16),
            vmem(tokens.shape, BF16),
            vmem((3, *block), BF16),
        ),
        in_specs=[in_hbm] * 7,
        out_specs=(in_vmem, in_vmem, in_vmem),
        scratch_shapes=[
            pltpu.SMEM(slots.shape, jnp.int32),
            pltpu.SMEM((1, 1, 3), jnp.int32),
            vmem((2, 2, features), BF16),
            vmem((2, 16, TILE), F32),
            vmem((nx, nz, 2, 16, TILE), BF16),
            vmem((3, *block), BF16),
            pltpu.SMEM((3, cap), jnp.int32),
            vmem((features, 2 * width), BF16),
            vmem((width, features), BF16),
            vmem((2, count * 8, TILE), F32),
            vmem((2, count * 8, TILE), F32),
            vmem((count, features), BF16),
            vmem((DT, count, TILE), BF16),
            vmem((DT, TILE, count), BF16),
            vmem((HT, TILE, count), BF16),
            vmem((3 * HT, count, TILE), BF16),
            vmem((2, nn, own, 3 * width), F32),
            vmem((2, nn, own, 3 * width), BF16),
            vmem((2, nn, own, 3 * width), BF16),
            vmem((2, nn, own, 3 * width), BF16),
            vmem((nx, nz, 2, 16, TILE), BF16),
            vmem((nx - 1, nz, 2, 16, TILE), BF16),
            vmem((nz, 2, 16, TILE), BF16),
            vmem((nz, 2, 16, TILE), BF16),
            dma((7,)),
            dma((nz,)),
            dma((nz,)),
            dma((nx - 1, nz)),
            dma((nx - 1, nz)),
            dma((2, nn)),
            dma((2, nn)),
            dma((2, nn)),
            dma((2, nn)),
            dma((nx - 1, nz)),
            dma((nx - 1, nz)),
            dma((nz,)),
            dma((nz,)),
        ],
        compiler_params=pltpu.CompilerParams(
            collective_id=0, has_side_effects=True, vmem_limit_bytes=VMEM_LIMIT
        ),
        name="pruned_layer",
    )(
        *[
            pltpu.with_memory_space_constraint(a, pltpu.HBM)
            for a in (
                slots, jnp.transpose(counts, (1, 2, 0)), tokens, cotangent,
                gate_tiles.reshape(block), up_tiles.reshape(block), down_tiles.reshape(block),
            )
        ]
    )
    layer_out, input_grad, *tile_grads = pl.pallas_call(
        write_kernel,
        out_shape=(
            jax.ShapeDtypeStruct(tokens.shape, BF16),
            jax.ShapeDtypeStruct(tokens.shape, BF16),
            *[jax.ShapeDtypeStruct(block, BF16)] * 3,
        ),
        in_specs=[in_vmem] * 3,
        out_specs=(anywhere,) * 5,
        scratch_shapes=[dma((5,))],
        compiler_params=pltpu.CompilerParams(vmem_limit_bytes=VMEM_LIMIT),
        name="write",
    )(*results)
    return (layer_out, input_grad, *(g[None, None] for g in tile_grads))


def solution(mesh, x_size=X_SIZE):
    tiles = P("narrow", "wide", None, None, None)
    panel = P("wide", "narrow")
    wide, narrow = mesh.shape["wide"], mesh.shape["narrow"]
    return jax.shard_map(
        functools.partial(per_device, wide // x_size, x_size, narrow),
        mesh=mesh,
        in_specs=(
            panel, panel, tiles, tiles, tiles,
            P(None, "narrow", "wide", None), P(None, "narrow", "wide"),
        ),
        out_specs=(panel, panel, tiles, tiles, tiles),
        check_vma=False,
    )
```

```python
import functools

import jax
import jax.numpy as jnp
from jax import lax
from jax.experimental import pallas as pl
from jax.experimental.pallas import tpu as pltpu
from jax.sharding import PartitionSpec as P

TILE = 128
HT = 3
DT = 8
LOC = HT * DT
X_SIZE = 4
VMEM_LIMIT = 24 * 1024 * 1024
F32, BF16 = jnp.float32, jnp.bfloat16
MESH = pl.DeviceIdType.MESH


def far_order(ring):
    return sorted(range(1, ring), key=lambda step: -min(step, ring - step))


def layer_kernel(
    nz, nx, nn, cap,
    slots_hbm, counts_hbm, tok_hbm, cot_hbm, gate_hbm, up_hbm, down_hbm,
    layer_out, input_grad, grads,
    slots, counts, own_in, pair, gathered, tiles, keys, w_in, w_down, rows, rows_out,
    tok, cot, tok_t, hid_t, act,
    part_own, part, part_in, acts, back, back_in, back_sum, last_in,
    sem_in, zs, zr, xs, xr, ps, pr, as_, ar, bs, br, ls, lr,
):
    wide, me = lax.axis_index("wide"), lax.axis_index("narrow")
    z, x = wide // nx, wide % nx
    half, reach = nz // 2, nz // 4
    width = HT * TILE
    features = DT * TILE
    tokens = 2 * nz * nx
    per_z = 2 * nx
    in_chunk = tokens // 2
    own_rows = in_chunk // nn
    home = reach - 1

    def at_z(step):
        return ((z + step + nz) % nz * nx + x, me)

    def at_x(step):
        return (z * nx + (x + step) % nx, me)

    def at_n(step):
        return (wide, (me + step) % nn)

    def slot_of(step):
        return (home + step + nz) % nz

    def remote(src, dst, send, recv, target):
        return pltpu.make_async_remote_copy(
            src_ref=src, dst_ref=dst, send_sem=send, recv_sem=recv,
            device_id=target, device_id_type=MESH,
        )

    barrier = pltpu.get_barrier_semaphore()
    z_near = sorted({s % nz for d in range(1, reach + 1) for s in (d, -d)})
    for step in z_near:
        pl.semaphore_signal(barrier, inc=1, device_id=at_z(step), device_id_type=MESH)
    for step in range(1, nx):
        pl.semaphore_signal(barrier, inc=1, device_id=at_x(step), device_id_type=MESH)
    for step in range(1, nn):
        pl.semaphore_signal(barrier, inc=1, device_id=at_n(step), device_id_type=MESH)

    loads = [
        pltpu.make_async_copy(tok_hbm, own_in.at[0], sem_in.at[0]),
        pltpu.make_async_copy(cot_hbm, own_in.at[1], sem_in.at[1]),
        pltpu.make_async_copy(gate_hbm, tiles.at[0], sem_in.at[2]),
        pltpu.make_async_copy(up_hbm, tiles.at[1], sem_in.at[3]),
        pltpu.make_async_copy(down_hbm, tiles.at[2], sem_in.at[4]),
        pltpu.make_async_copy(slots_hbm, slots, sem_in.at[5]),
        pltpu.make_async_copy(counts_hbm, counts, sem_in.at[6]),
    ]
    for load in loads:
        load.start()

    loads[0].wait()
    loads[1].wait()
    for o in range(2):
        both = own_in[o].astype(F32)
        for k in range(DT):
            for i in range(2):
                pair[o, pl.ds(8 * i + k, 1), :] = both[i : i + 1, k * TILE : (k + 1) * TILE]
        gathered[x, home, o] = pair[o].astype(BF16)

    pl.semaphore_wait(barrier, len(z_near) + nx - 1 + nn - 1)

    def z_copy(slot, step):
        to_slot = (slot - step + nz) % nz
        return remote(
            gathered.at[x, slot], gathered.at[x, to_slot],
            zs.at[to_slot], zr.at[to_slot], at_z(step),
        )

    def z_arrival(slot):
        return remote(
            gathered.at[x, slot], gathered.at[x, slot], zs.at[slot], zr.at[slot], at_z(1),
        )

    def x_copy(slot, step):
        return remote(
            gathered.at[x, slot], gathered.at[x, slot],
            xs.at[step - 1, slot], xr.at[step - 1, slot], at_x(step),
        )

    for d in range(1, reach + 1):
        z_copy(home, d).start()
        z_copy(home, -d).start()
    for step in far_order(nx):
        x_copy(home, step).start()

    def relay(d, carry):
        behind = slot_of(-d)
        z_arrival(behind).wait_recv()

        @pl.when(d + reach <= half)
        def _():
            z_copy(behind, reach).start()

        @pl.when(d < half)
        def _():
            ahead = slot_of(d)
            z_arrival(ahead).wait_recv()

            @pl.when(d + reach < half)
            def _():
                z_copy(ahead, -reach).start()

            for step in far_order(nx):
                x_copy(ahead, step).start()

        for step in far_order(nx):
            x_copy(behind, step).start()
        return carry

    for load in loads[2:]:
        load.wait()
    for m in range(3):
        for s in range(cap):
            keys[m, s] = jnp.where(s < counts[0, 0, m], slots[m, 0, 0, s], -1)

    def place(m, p, carry):
        found = jnp.int32(-1)
        for s in range(cap):
            found = jnp.where(keys[m, s] == p, s, found)
        live = found >= 0
        tile = tiles[m, jnp.where(live, found, 0)]
        tile = jnp.where(live, tile, jnp.zeros_like(tile))
        if m < 2:
            w_in[
                pl.ds(pl.multiple_of(p // HT * TILE, TILE), TILE),
                pl.ds(pl.multiple_of(p % HT * TILE + m * width, TILE), TILE),
            ] = tile
        else:
            w_down[
                pl.ds(pl.multiple_of(p // DT * TILE, TILE), TILE),
                pl.ds(pl.multiple_of(p % DT * TILE, TILE), TILE),
            ] = tile
        return carry

    def unpack(c):
        def one(slot, carry):
            for step in range(1, nx):
                x_copy(slot, step).wait_recv()
            for o in range(2):
                for xx in range(nx):
                    at = pl.multiple_of(slot * 8 * per_z + xx * 16, 16)
                    rows[o, pl.ds(at, 16), :] = gathered[xx, slot, o].astype(F32)
            return carry

        lax.fori_loop(c * half, (c + 1) * half, one, 0)
        here = pl.ds(c * in_chunk, in_chunk)
        for k in range(DT):
            picked = pl.ds(c * in_chunk * 8 + k, in_chunk, stride=8)
            tok[here, k * TILE : (k + 1) * TILE] = rows[0, picked, :].astype(BF16)
            cot[k, here, :] = rows[1, picked, :].astype(BF16)

    def p_copy(c, step):
        return remote(
            part.at[c, (me + step) % nn], part_in.at[c, step],
            ps.at[c, step], pr.at[c, step], at_n(step),
        )

    def front(c):
        here = pl.ds(c * in_chunk, in_chunk)
        gate_up = jnp.dot(tok[here, :], w_in[...], preferred_element_type=F32)
        hid = jnp.zeros((in_chunk, width), F32)
        for k in range(DT):
            hid = hid + lax.dot_general(
                cot[k, here, :], w_down[:, k * TILE : (k + 1) * TILE],
                (((1,), (1,)), ((), ())), preferred_element_type=F32,
            )
        for value, at in ((gate_up, 0), (hid, 2 * width)):
            value = value.reshape(nn, own_rows, value.shape[1])
            part_own[c, :, :, at : at + value.shape[2]] = value
            part[c, :, :, at : at + value.shape[2]] = value.astype(BF16)
        for step in far_order(nn):
            p_copy(c, step).start()

    def a_copy(c, step):
        return remote(
            acts.at[c, me], acts.at[c, me], as_.at[c, step], ar.at[c, step], at_n(step),
        )

    def middle(c):
        total = part_own[c, me]
        for step in range(1, nn):
            p_copy(c, step).wait_recv()
            total = total + part_in[c, step].astype(F32)
        gate_sum, up_sum = total[:, :width], total[:, width : 2 * width]
        hidden_grad = total[:, 2 * width :]
        sig = jax.nn.sigmoid(gate_sum)
        acts[c, me, :, :width] = (gate_sum * sig * up_sum).astype(BF16)
        acts[c, me, :, width : 2 * width] = (
            hidden_grad * up_sum * sig * (1.0 + gate_sum * (1.0 - sig))
        ).astype(BF16)
        acts[c, me, :, 2 * width :] = (hidden_grad * gate_sum * sig).astype(BF16)
        for step in far_order(nn):
            a_copy(c, step).start()

    def b_copy(slot, step):
        return remote(
            back.at[(x + step) % nx, slot], back_in.at[step - 1, slot],
            bs.at[step - 1, slot], br.at[step - 1, slot], at_x(step),
        )

    def far_first(c, q):
        d = half - c_start(c) - (q + 1) // 2
        return slot_of(jnp.where(q % 2 == 0, d, nz - d))

    def c_start(c):
        return 0 if c else reach

    def finish(c):
        here = pl.ds(c * in_chunk, in_chunk)
        for step in range(1, nn):
            a_copy(c, step).wait_recv()
        everything = acts[c].astype(F32).reshape(in_chunk, 3 * width).astype(BF16)
        for j in range(3 * HT):
            act[j, here, :] = everything[:, j * TILE : (j + 1) * TILE]
        out = jnp.dot(everything[:, :width], w_down[...], preferred_element_type=F32)
        both_act = everything[:, width:]
        for k in range(DT):
            picked = pl.ds(c * in_chunk * 8 + k, in_chunk, stride=8)
            rows_out[0, picked, :] = out[:, k * TILE : (k + 1) * TILE]
            rows_out[1, picked, :] = lax.dot_general(
                both_act, w_in[k * TILE : (k + 1) * TILE, :],
                (((1,), (1,)), ((), ())), preferred_element_type=F32,
            )

        def to_x(q, carry):
            slot = far_first(c, q)
            for o in range(2):
                for xx in range(nx):
                    at = pl.multiple_of(slot * 8 * per_z + xx * 16, 16)
                    back[xx, slot, o] = rows_out[o, pl.ds(at, 16), :].astype(BF16)
            for step in far_order(nx):
                b_copy(slot, step).start()
            return carry

        lax.fori_loop(0, half, to_x, 0)

    def l_copy(slot):
        step = slot - home
        to_slot = slot_of(-step)
        return remote(
            back_sum.at[slot], last_in.at[to_slot], ls.at[slot], lr.at[to_slot], at_z(step),
        )

    def l_arrival(slot):
        return remote(
            back_sum.at[slot], last_in.at[slot], ls.at[slot], lr.at[slot], at_z(1),
        )

    def summed_over_x(slot):
        for step in range(1, nx):
            b_copy(slot, step).wait_recv()
        at = pl.multiple_of(slot * 8 * per_z + x * 16, 16)
        total = rows_out[:, pl.ds(at, 16), :]
        for step in range(1, nx):
            total = total + back_in[step - 1, slot].astype(F32)
        return total

    def to_z(c):
        def one(q, carry):
            slot = far_first(c, q)
            back_sum[slot] = summed_over_x(slot).astype(BF16)
            l_copy(slot).start()
            return carry

        lax.fori_loop(0, half if c else half - 1, one, 0)

    split = reach + (half - reach) // 2
    lax.fori_loop(0, LOC // 2, functools.partial(place, 0), 0)
    lax.fori_loop(1, reach + 1, relay, 0)
    lax.fori_loop(LOC // 2, LOC, functools.partial(place, 0), 0)
    lax.fori_loop(0, LOC, functools.partial(place, 1), 0)
    lax.fori_loop(0, LOC, functools.partial(place, 2), 0)
    lax.fori_loop(reach + 1, split + 1, relay, 0)
    unpack(0)
    front(0)
    lax.fori_loop(split + 1, half + 1, relay, 0)
    unpack(1)
    front(1)
    middle(0)
    middle(1)
    finish(0)
    finish(1)
    to_z(0)
    to_z(1)
    for k in range(DT):
        tok_t[k] = rows[0, pl.ds(k, tokens, stride=8), :].T.astype(BF16)

    for j in range(HT):
        hid_t[j] = act[j].astype(F32).T.astype(BF16)
    for m in range(3):

        def tile_grad(s, carry):
            p = slots[m, 0, 0, s]
            if m < 2:
                left, right = tok_t[p // HT], act[HT * (m + 1) + p % HT]
            else:
                left, right = hid_t[p // DT], cot[p % DT]
            grad = jnp.dot(left, right, preferred_element_type=F32)
            live = (s < counts[0, 0, m]).astype(F32)
            grads[m, s] = (grad * live).astype(BF16)
            return carry

        lax.fori_loop(0, cap, tile_grad, 0, unroll=4)

    def last(slot, carry):
        l_arrival(slot).wait_recv()
        return carry + last_in[slot].astype(F32)

    final = lax.fori_loop(0, home, last, summed_over_x(home))
    final = lax.fori_loop(home + 1, nz, last, final)
    for o, to in ((0, layer_out), (1, input_grad)):
        pair[o] = final[o]
        for k in range(DT):
            for i in range(2):
                to[i : i + 1, k * TILE : (k + 1) * TILE] = pair[
                    o, pl.ds(8 * i + k, 1), :
                ].astype(BF16)

    def sent(slot, carry):
        for step in range(1, nx):
            x_copy(slot, step).wait_send()
            b_copy(slot, step).wait_send()

        @pl.when(slot != home)
        def _():
            z_arrival(slot).wait_send()
            l_copy(slot).wait_send()

        return carry

    lax.fori_loop(0, nz, sent, 0)
    for c in range(2):
        for step in range(1, nn):
            p_copy(c, step).wait_send()
            a_copy(c, step).wait_send()


def write_kernel(*refs):
    sems = refs[-1]
    layer_out, input_grad, grads, *outs = refs[:-1]
    sources = (layer_out, input_grad, grads.at[0], grads.at[1], grads.at[2])
    stores = [
        pltpu.make_async_copy(source, to, sems.at[i])
        for i, (source, to) in enumerate(zip(sources, outs))
    ]
    for store in stores:
        store.start()
    for store in stores:
        store.wait()


def per_device(nz, nx, nn, tokens, cotangent, gate_tiles, up_tiles, down_tiles, slots, counts):
    cap = gate_tiles.shape[2]
    count = 2 * nz * nx
    own = count // 2 // nn
    block = (cap, TILE, TILE)
    width = HT * TILE
    features = DT * TILE
    dma = pltpu.SemaphoreType.DMA
    vmem = pltpu.VMEM
    anywhere = pl.BlockSpec(memory_space=pl.ANY)
    in_hbm = pl.BlockSpec(memory_space=pltpu.HBM)
    in_vmem = pl.BlockSpec(memory_space=pltpu.VMEM)
    results = pl.pallas_call(
        functools.partial(layer_kernel, nz, nx, nn, cap),
        out_shape=(
            vmem(tokens.shape, BF16),
            vmem(tokens.shape, BF16),
            vmem((3, *block), BF16),
        ),
        in_specs=[in_hbm] * 7,
        out_specs=(in_vmem, in_vmem, in_vmem),
        scratch_shapes=[
            pltpu.SMEM(slots.shape, jnp.int32),
            pltpu.SMEM((1, 1, 3), jnp.int32),
            vmem((2, 2, features), BF16),
            vmem((2, 16, TILE), F32),
            vmem((nx, nz, 2, 16, TILE), BF16),
            vmem((3, *block), BF16),
            pltpu.SMEM((3, cap), jnp.int32),
            vmem((features, 2 * width), BF16),
            vmem((width, features), BF16),
            vmem((2, count * 8, TILE), F32),
            vmem((2, count * 8, TILE), F32),
            vmem((count, features), BF16),
            vmem((DT, count, TILE), BF16),
            vmem((DT, TILE, count), BF16),
            vmem((HT, TILE, count), BF16),
            vmem((3 * HT, count, TILE), BF16),
            vmem((2, nn, own, 3 * width), F32),
            vmem((2, nn, own, 3 * width), BF16),
            vmem((2, nn, own, 3 * width), BF16),
            vmem((2, nn, own, 3 * width), BF16),
            vmem((nx, nz, 2, 16, TILE), BF16),
            vmem((nx - 1, nz, 2, 16, TILE), BF16),
            vmem((nz, 2, 16, TILE), BF16),
            vmem((nz, 2, 16, TILE), BF16),
            dma((7,)),
            dma((nz,)),
            dma((nz,)),
            dma((nx - 1, nz)),
            dma((nx - 1, nz)),
            dma((2, nn)),
            dma((2, nn)),
            dma((2, nn)),
            dma((2, nn)),
            dma((nx - 1, nz)),
            dma((nx - 1, nz)),
            dma((nz,)),
            dma((nz,)),
        ],
        compiler_params=pltpu.CompilerParams(
            collective_id=0, has_side_effects=True, vmem_limit_bytes=VMEM_LIMIT
        ),
        name="pruned_layer",
    )(
        *[
            pltpu.with_memory_space_constraint(a, pltpu.HBM)
            for a in (
                slots, jnp.transpose(counts, (1, 2, 0)), tokens, cotangent,
                gate_tiles.reshape(block), up_tiles.reshape(block), down_tiles.reshape(block),
            )
        ]
    )
    layer_out, input_grad, *tile_grads = pl.pallas_call(
        write_kernel,
        out_shape=(
            jax.ShapeDtypeStruct(tokens.shape, BF16),
            jax.ShapeDtypeStruct(tokens.shape, BF16),
            *[jax.ShapeDtypeStruct(block, BF16)] * 3,
        ),
        in_specs=[in_vmem] * 3,
        out_specs=(anywhere,) * 5,
        scratch_shapes=[dma((5,))],
        compiler_params=pltpu.CompilerParams(vmem_limit_bytes=VMEM_LIMIT),
        name="write",
    )(*results)
    return (layer_out, input_grad, *(g[None, None] for g in tile_grads))


def solution(mesh, x_size=X_SIZE):
    tiles = P("narrow", "wide", None, None, None)
    panel = P("wide", "narrow")
    wide, narrow = mesh.shape["wide"], mesh.shape["narrow"]
    return jax.shard_map(
        functools.partial(per_device, wide // x_size, x_size, narrow),
        mesh=mesh,
        in_specs=(
            panel, panel, tiles, tiles, tiles,
            P(None, "narrow", "wide", None), P(None, "narrow", "wide"),
        ),
        out_specs=(panel, panel, tiles, tiles, tiles),
        check_vma=False,
    )
```

```python
import functools

import jax
import jax.numpy as jnp
from jax import lax
from jax.experimental import pallas as pl
from jax.experimental.pallas import tpu as pltpu
from jax.sharding import PartitionSpec as P

TILE = 128
HT = 3
DT = 8
LOC = HT * DT
X_SIZE = 4
VMEM_LIMIT = 24 * 1024 * 1024
F32, BF16 = jnp.float32, jnp.bfloat16
MESH = pl.DeviceIdType.MESH


def far_order(ring):
    return sorted(range(1, ring), key=lambda step: -min(step, ring - step))


def layer_kernel(
    nz, nx, nn, cap,
    slots_hbm, counts_hbm, tok_hbm, cot_hbm, gate_hbm, up_hbm, down_hbm,
    layer_out, input_grad, grads,
    slots, counts, own_in, pair, gathered, tiles, keys, w_in, w_down, rows, rows_out,
    tok, cot, tok_t, hid_t, act,
    part_own, part, part_in, acts, back, back_in, back_sum, last_in,
    sem_in, zs, zr, xs, xr, ps, pr, as_, ar, bs, br, ls, lr,
):
    wide, me = lax.axis_index("wide"), lax.axis_index("narrow")
    z, x = wide // nx, wide % nx
    half, reach = nz // 2, nz // 4
    width = HT * TILE
    features = DT * TILE
    tokens = 2 * nz * nx
    per_z = 2 * nx
    in_chunk = tokens // 2
    own_rows = in_chunk // nn
    home = reach - 1

    def at_z(step):
        return ((z + step + nz) % nz * nx + x, me)

    def at_x(step):
        return (z * nx + (x + step) % nx, me)

    def at_n(step):
        return (wide, (me + step) % nn)

    def slot_of(step):
        return (home + step + nz) % nz

    def remote(src, dst, send, recv, target):
        return pltpu.make_async_remote_copy(
            src_ref=src, dst_ref=dst, send_sem=send, recv_sem=recv,
            device_id=target, device_id_type=MESH,
        )

    barrier = pltpu.get_barrier_semaphore()
    z_near = sorted({s % nz for d in range(1, reach + 1) for s in (d, -d)})
    for step in z_near:
        pl.semaphore_signal(barrier, inc=1, device_id=at_z(step), device_id_type=MESH)
    for step in range(1, nx):
        pl.semaphore_signal(barrier, inc=1, device_id=at_x(step), device_id_type=MESH)
    for step in range(1, nn):
        pl.semaphore_signal(barrier, inc=1, device_id=at_n(step), device_id_type=MESH)

    loads = [
        pltpu.make_async_copy(tok_hbm, own_in.at[0], sem_in.at[0]),
        pltpu.make_async_copy(cot_hbm, own_in.at[1], sem_in.at[1]),
        pltpu.make_async_copy(gate_hbm, tiles.at[0], sem_in.at[2]),
        pltpu.make_async_copy(up_hbm, tiles.at[1], sem_in.at[3]),
        pltpu.make_async_copy(down_hbm, tiles.at[2], sem_in.at[4]),
        pltpu.make_async_copy(slots_hbm, slots, sem_in.at[5]),
        pltpu.make_async_copy(counts_hbm, counts, sem_in.at[6]),
    ]
    for load in loads:
        load.start()

    loads[0].wait()
    loads[1].wait()
    for o in range(2):
        both = own_in[o].astype(F32)
        for k in range(DT):
            for i in range(2):
                pair[o, pl.ds(8 * i + k, 1), :] = both[i : i + 1, k * TILE : (k + 1) * TILE]
        gathered[x, home, o] = pair[o].astype(BF16)

    pl.semaphore_wait(barrier, len(z_near) + nx - 1 + nn - 1)

    def z_copy(slot, step):
        to_slot = (slot - step + nz) % nz
        return remote(
            gathered.at[x, slot], gathered.at[x, to_slot],
            zs.at[to_slot], zr.at[to_slot], at_z(step),
        )

    def z_arrival(slot):
        return remote(
            gathered.at[x, slot], gathered.at[x, slot], zs.at[slot], zr.at[slot], at_z(1),
        )

    def x_copy(slot, step):
        return remote(
            gathered.at[x, slot], gathered.at[x, slot],
            xs.at[step - 1, slot], xr.at[step - 1, slot], at_x(step),
        )

    for d in range(reach, 0, -1):
        z_copy(home, d).start()
        z_copy(home, -d).start()
    for step in far_order(nx):
        x_copy(home, step).start()

    def relay(d, carry):
        behind = slot_of(-d)
        z_arrival(behind).wait_recv()

        @pl.when(d + reach <= half)
        def _():
            z_copy(behind, reach).start()

        @pl.when(d < half)
        def _():
            ahead = slot_of(d)
            z_arrival(ahead).wait_recv()

            @pl.when(d + reach < half)
            def _():
                z_copy(ahead, -reach).start()

            for step in far_order(nx):
                x_copy(ahead, step).start()

        for step in far_order(nx):
            x_copy(behind, step).start()
        return carry

    for load in loads[2:]:
        load.wait()
    for m in range(3):
        for s in range(cap):
            keys[m, s] = jnp.where(s < counts[0, 0, m], slots[m, 0, 0, s], -1)

    def place(m, p, carry):
        found = jnp.int32(-1)
        for s in range(cap):
            found = jnp.where(keys[m, s] == p, s, found)
        live = found >= 0
        tile = tiles[m, jnp.where(live, found, 0)]
        tile = jnp.where(live, tile, jnp.zeros_like(tile))
        if m < 2:
            w_in[
                pl.ds(pl.multiple_of(p // HT * TILE, TILE), TILE),
                pl.ds(pl.multiple_of(p % HT * TILE + m * width, TILE), TILE),
            ] = tile
        else:
            w_down[
                pl.ds(pl.multiple_of(p // DT * TILE, TILE), TILE),
                pl.ds(pl.multiple_of(p % DT * TILE, TILE), TILE),
            ] = tile
        return carry

    def unpack(c):
        def one(slot, carry):
            for step in range(1, nx):
                x_copy(slot, step).wait_recv()
            for o in range(2):
                for xx in range(nx):
                    at = pl.multiple_of(slot * 8 * per_z + xx * 16, 16)
                    rows[o, pl.ds(at, 16), :] = gathered[xx, slot, o].astype(F32)
            return carry

        lax.fori_loop(c * half, (c + 1) * half, one, 0)
        here = pl.ds(c * in_chunk, in_chunk)
        for k in range(DT):
            picked = pl.ds(c * in_chunk * 8 + k, in_chunk, stride=8)
            tok[here, k * TILE : (k + 1) * TILE] = rows[0, picked, :].astype(BF16)
            cot[k, here, :] = rows[1, picked, :].astype(BF16)

    def p_copy(c, step):
        return remote(
            part.at[c, (me + step) % nn], part_in.at[c, step],
            ps.at[c, step], pr.at[c, step], at_n(step),
        )

    def front(c):
        here = pl.ds(c * in_chunk, in_chunk)
        gate_up = jnp.dot(tok[here, :], w_in[...], preferred_element_type=F32)
        hid = jnp.zeros((in_chunk, width), F32)
        for k in range(DT):
            hid = hid + lax.dot_general(
                cot[k, here, :], w_down[:, k * TILE : (k + 1) * TILE],
                (((1,), (1,)), ((), ())), preferred_element_type=F32,
            )
        for value, at in ((gate_up, 0), (hid, 2 * width)):
            value = value.reshape(nn, own_rows, value.shape[1])
            part_own[c, :, :, at : at + value.shape[2]] = value
            part[c, :, :, at : at + value.shape[2]] = value.astype(BF16)
        for step in far_order(nn):
            p_copy(c, step).start()

    def a_copy(c, step):
        return remote(
            acts.at[c, me], acts.at[c, me], as_.at[c, step], ar.at[c, step], at_n(step),
        )

    def middle(c):
        total = part_own[c, me]
        for step in range(1, nn):
            p_copy(c, step).wait_recv()
            total = total + part_in[c, step].astype(F32)
        gate_sum, up_sum = total[:, :width], total[:, width : 2 * width]
        hidden_grad = total[:, 2 * width :]
        sig = jax.nn.sigmoid(gate_sum)
        acts[c, me, :, :width] = (gate_sum * sig * up_sum).astype(BF16)
        acts[c, me, :, width : 2 * width] = (
            hidden_grad * up_sum * sig * (1.0 + gate_sum * (1.0 - sig))
        ).astype(BF16)
        acts[c, me, :, 2 * width :] = (hidden_grad * gate_sum * sig).astype(BF16)
        for step in far_order(nn):
            a_copy(c, step).start()

    def b_copy(slot, step):
        return remote(
            back.at[(x + step) % nx, slot], back_in.at[step - 1, slot],
            bs.at[step - 1, slot], br.at[step - 1, slot], at_x(step),
        )

    def far_first(c, q):
        d = half - c_start(c) - (q + 1) // 2
        return slot_of(jnp.where(q % 2 == 0, d, nz - d))

    def c_start(c):
        return 0 if c else reach

    def finish(c):
        here = pl.ds(c * in_chunk, in_chunk)
        for step in range(1, nn):
            a_copy(c, step).wait_recv()
        everything = acts[c].astype(F32).reshape(in_chunk, 3 * width).astype(BF16)
        for j in range(3 * HT):
            act[j, here, :] = everything[:, j * TILE : (j + 1) * TILE]
        out = jnp.dot(everything[:, :width], w_down[...], preferred_element_type=F32)
        both_act = everything[:, width:]
        for k in range(DT):
            picked = pl.ds(c * in_chunk * 8 + k, in_chunk, stride=8)
            rows_out[0, picked, :] = out[:, k * TILE : (k + 1) * TILE]
            rows_out[1, picked, :] = lax.dot_general(
                both_act, w_in[k * TILE : (k + 1) * TILE, :],
                (((1,), (1,)), ((), ())), preferred_element_type=F32,
            )

        def to_x(q, carry):
            slot = far_first(c, q)
            for o in range(2):
                for xx in range(nx):
                    at = pl.multiple_of(slot * 8 * per_z + xx * 16, 16)
                    back[xx, slot, o] = rows_out[o, pl.ds(at, 16), :].astype(BF16)
            for step in far_order(nx):
                b_copy(slot, step).start()
            return carry

        lax.fori_loop(0, half, to_x, 0)

    def l_copy(slot):
        step = slot - home
        to_slot = slot_of(-step)
        return remote(
            back_sum.at[slot], last_in.at[to_slot], ls.at[slot], lr.at[to_slot], at_z(step),
        )

    def l_arrival(slot):
        return remote(
            back_sum.at[slot], last_in.at[slot], ls.at[slot], lr.at[slot], at_z(1),
        )

    def summed_over_x(slot):
        for step in range(1, nx):
            b_copy(slot, step).wait_recv()
        at = pl.multiple_of(slot * 8 * per_z + x * 16, 16)
        total = rows_out[:, pl.ds(at, 16), :]
        for step in range(1, nx):
            total = total + back_in[step - 1, slot].astype(F32)
        return total

    def to_z(c):
        def one(q, carry):
            slot = far_first(c, q)
            back_sum[slot] = summed_over_x(slot).astype(BF16)
            l_copy(slot).start()
            return carry

        lax.fori_loop(0, half if c else half - 1, one, 0)

    split = reach + (half - reach) // 2
    lax.fori_loop(0, LOC // 2, functools.partial(place, 0), 0)
    lax.fori_loop(1, reach + 1, relay, 0)
    lax.fori_loop(LOC // 2, LOC, functools.partial(place, 0), 0)
    lax.fori_loop(0, LOC, functools.partial(place, 1), 0)
    lax.fori_loop(0, LOC, functools.partial(place, 2), 0)
    lax.fori_loop(reach + 1, split + 1, relay, 0)
    unpack(0)
    front(0)
    lax.fori_loop(split + 1, half + 1, relay, 0)
    unpack(1)
    front(1)
    middle(0)
    middle(1)
    finish(0)
    finish(1)
    to_z(0)
    to_z(1)
    for k in range(DT):
        tok_t[k] = rows[0, pl.ds(k, tokens, stride=8), :].T.astype(BF16)

    for j in range(HT):
        hid_t[j] = act[j].astype(F32).T.astype(BF16)
    for m in range(3):

        def tile_grad(s, carry):
            p = slots[m, 0, 0, s]
            if m < 2:
                left, right = tok_t[p // HT], act[HT * (m + 1) + p % HT]
            else:
                left, right = hid_t[p // DT], cot[p % DT]
            grad = jnp.dot(left, right, preferred_element_type=F32)
            live = (s < counts[0, 0, m]).astype(F32)
            grads[m, s] = (grad * live).astype(BF16)
            return carry

        lax.fori_loop(0, cap, tile_grad, 0, unroll=4)

    def last(slot, carry):
        l_arrival(slot).wait_recv()
        return carry + last_in[slot].astype(F32)

    final = lax.fori_loop(0, home, last, summed_over_x(home))
    final = lax.fori_loop(home + 1, nz, last, final)
    for o, to in ((0, layer_out), (1, input_grad)):
        pair[o] = final[o]
        for k in range(DT):
            for i in range(2):
                to[i : i + 1, k * TILE : (k + 1) * TILE] = pair[
                    o, pl.ds(8 * i + k, 1), :
                ].astype(BF16)

    def sent(slot, carry):
        for step in range(1, nx):
            x_copy(slot, step).wait_send()
            b_copy(slot, step).wait_send()

        @pl.when(slot != home)
        def _():
            z_arrival(slot).wait_send()
            l_copy(slot).wait_send()

        return carry

    lax.fori_loop(0, nz, sent, 0)
    for c in range(2):
        for step in range(1, nn):
            p_copy(c, step).wait_send()
            a_copy(c, step).wait_send()


def write_kernel(*refs):
    sems = refs[-1]
    layer_out, input_grad, grads, *outs = refs[:-1]
    sources = (layer_out, input_grad, grads.at[0], grads.at[1], grads.at[2])
    stores = [
        pltpu.make_async_copy(source, to, sems.at[i])
        for i, (source, to) in enumerate(zip(sources, outs))
    ]
    for store in stores:
        store.start()
    for store in stores:
        store.wait()


def per_device(nz, nx, nn, tokens, cotangent, gate_tiles, up_tiles, down_tiles, slots, counts):
    cap = gate_tiles.shape[2]
    count = 2 * nz * nx
    own = count // 2 // nn
    block = (cap, TILE, TILE)
    width = HT * TILE
    features = DT * TILE
    dma = pltpu.SemaphoreType.DMA
    vmem = pltpu.VMEM
    anywhere = pl.BlockSpec(memory_space=pl.ANY)
    in_hbm = pl.BlockSpec(memory_space=pltpu.HBM)
    in_vmem = pl.BlockSpec(memory_space=pltpu.VMEM)
    results = pl.pallas_call(
        functools.partial(layer_kernel, nz, nx, nn, cap),
        out_shape=(
            vmem(tokens.shape, BF16),
            vmem(tokens.shape, BF16),
            vmem((3, *block), BF16),
        ),
        in_specs=[in_hbm] * 7,
        out_specs=(in_vmem, in_vmem, in_vmem),
        scratch_shapes=[
            pltpu.SMEM(slots.shape, jnp.int32),
            pltpu.SMEM((1, 1, 3), jnp.int32),
            vmem((2, 2, features), BF16),
            vmem((2, 16, TILE), F32),
            vmem((nx, nz, 2, 16, TILE), BF16),
            vmem((3, *block), BF16),
            pltpu.SMEM((3, cap), jnp.int32),
            vmem((features, 2 * width), BF16),
            vmem((width, features), BF16),
            vmem((2, count * 8, TILE), F32),
            vmem((2, count * 8, TILE), F32),
            vmem((count, features), BF16),
            vmem((DT, count, TILE), BF16),
            vmem((DT, TILE, count), BF16),
            vmem((HT, TILE, count), BF16),
            vmem((3 * HT, count, TILE), BF16),
            vmem((2, nn, own, 3 * width), F32),
            vmem((2, nn, own, 3 * width), BF16),
            vmem((2, nn, own, 3 * width), BF16),
            vmem((2, nn, own, 3 * width), BF16),
            vmem((nx, nz, 2, 16, TILE), BF16),
            vmem((nx - 1, nz, 2, 16, TILE), BF16),
            vmem((nz, 2, 16, TILE), BF16),
            vmem((nz, 2, 16, TILE), BF16),
            dma((7,)),
            dma((nz,)),
            dma((nz,)),
            dma((nx - 1, nz)),
            dma((nx - 1, nz)),
            dma((2, nn)),
            dma((2, nn)),
            dma((2, nn)),
            dma((2, nn)),
            dma((nx - 1, nz)),
            dma((nx - 1, nz)),
            dma((nz,)),
            dma((nz,)),
        ],
        compiler_params=pltpu.CompilerParams(
            collective_id=0, has_side_effects=True, vmem_limit_bytes=VMEM_LIMIT
        ),
        name="pruned_layer",
    )(
        *[
            pltpu.with_memory_space_constraint(a, pltpu.HBM)
            for a in (
                slots, jnp.transpose(counts, (1, 2, 0)), tokens, cotangent,
                gate_tiles.reshape(block), up_tiles.reshape(block), down_tiles.reshape(block),
            )
        ]
    )
    layer_out, input_grad, *tile_grads = pl.pallas_call(
        write_kernel,
        out_shape=(
            jax.ShapeDtypeStruct(tokens.shape, BF16),
            jax.ShapeDtypeStruct(tokens.shape, BF16),
            *[jax.ShapeDtypeStruct(block, BF16)] * 3,
        ),
        in_specs=[in_vmem] * 3,
        out_specs=(anywhere,) * 5,
        scratch_shapes=[dma((5,))],
        compiler_params=pltpu.CompilerParams(vmem_limit_bytes=VMEM_LIMIT),
        name="write",
    )(*results)
    return (layer_out, input_grad, *(g[None, None] for g in tile_grads))


def solution(mesh, x_size=X_SIZE):
    tiles = P("narrow", "wide", None, None, None)
    panel = P("wide", "narrow")
    wide, narrow = mesh.shape["wide"], mesh.shape["narrow"]
    return jax.shard_map(
        functools.partial(per_device, wide // x_size, x_size, narrow),
        mesh=mesh,
        in_specs=(
            panel, panel, tiles, tiles, tiles,
            P(None, "narrow", "wide", None), P(None, "narrow", "wide"),
        ),
        out_specs=(panel, panel, tiles, tiles, tiles),
        check_vma=False,
    )
```
